32 devices in a mesh: seq: 8 (over z, x), ch: 4 (over y, core).
Axes of the slice: x: 2, y: 2, z: 4, core: 2. Of those that a mesh axis runs over, the one named last changes fastest.
Arguments:
- query_raw: bfloat16 [1024, 2048], P('seq', 'ch'), may hold values from -6 to 6
- key_raw: bfloat16 [1024, 2048], P('seq', 'ch'), may hold values from -6 to 6
- value_raw: bfloat16 [1024, 2048], P('seq', 'ch'), may hold values from -6 to 6
- featurizer: float32 [3, 7, 2048], P(None, None, 'ch'), may hold values from -2 to 2
- filter_taps: bfloat16 [1024, 2048], P(('seq', 'ch')), may hold values from -2.5 to 2.5
- cotangent: bfloat16 [1024, 2048], P('seq', 'ch'), may hold values from -6 to 6
Outputs:
- mixed: bfloat16 [1024, 2048], P('seq', 'ch')
- query_grad: bfloat16 [1024, 2048], P('seq', 'ch')
- key_grad: bfloat16 [1024, 2048], P('seq', 'ch')
- value_grad: bfloat16 [1024, 2048], P('seq', 'ch')
- filter_grad: float32 [1024, 2048], P(('seq', 'ch'))
- featurizer_grad: float32 [3, 7, 2048], P(None, None, 'ch')
The draws below stay inside these ranges and needn't reach their ends.
All inputs are finite; a program needn't handle non-finite values.
Results may differ from the reference program's by a relative error of at most 0.0085.
Values may be sent and summed in bfloat16 or wider, within the bound.
A program may use at most 64 MiB of HBM per device.

```python
import math
import jax
import jax.numpy as jnp
from jax import lax

D = 2048
TAPS = 7
TOKENS = 1024


def draw_filter_taps(key, part):
    base = jax.random.fold_in(key, 7)
    noise_key, rate_key, pick_key, amp_key = jax.random.split(base, 4)
    positions = jnp.arange(TOKENS, dtype=jnp.float32)
    slow_rate = math.log(10.0) / TOKENS
    slow_rates = slow_rate * jnp.exp(jax.random.uniform(rate_key, (D,), jnp.float32, math.log(0.25), 0.0))
    fast_rates = jnp.exp(jax.random.uniform(jax.random.fold_in(rate_key, 3), (D,), jnp.float32, math.log(1.0 / 50.0), math.log(1.0 / 30.0)))
    picked = jax.random.bernoulli(pick_key, 0.5, (D,))
    rates = jnp.where(picked, slow_rates, fast_rates)
    noise = jax.random.truncated_normal(noise_key, -4.0, 4.0, (TOKENS, D), jnp.float32)
    amplitude = jnp.sqrt((1.0 - jnp.exp(-2.0 * rates)) / (1.0 - jnp.exp(-2.0 * rates * TOKENS)))
    amplitude = amplitude * jnp.exp(jax.random.uniform(amp_key, (D,), jnp.float32, math.log(0.5), math.log(2.0)))
    taps = noise * amplitude[None, :] * jnp.exp(-rates[None, :] * positions[:, None])
    return taps.astype(jnp.bfloat16)


def levels(own_key, shape, pieces, least, top_value):
    factor_of = 1.0
    for dim, shards_of in pieces:
        draws = jax.random.uniform(jax.random.fold_in(jax.random.fold_in(own_key, 6), dim), (shards_of,), jnp.float32, least / len(pieces), top_value / len(pieces))
        factor_of = factor_of * jnp.repeat(jnp.exp(draws), shape[dim] // shards_of).reshape((-1,) + (1,) * (len(shape) - 1 - dim))
    return factor_of


def normal_values(own_key, dims, spread, bound, cuts=(), kind=jnp.bfloat16):
    entries = spread * jax.random.normal(own_key, dims, jnp.float32)
    if cuts:
        entries = entries * levels(own_key, dims, cuts, -0.22, 0.18)
    return jnp.clip(entries, -bound, bound).astype(kind)


def setup_inputs(seed: int = 0) -> dict:
    splits = jax.random.split(jax.random.key(seed), 7)
    query_raw = normal_values(splits[0], (TOKENS, D), 1.0, 6.0, ((0, 8), (1, 4)))
    key_raw = normal_values(splits[1], (TOKENS, D), 1.0, 6.0, ((0, 8), (1, 4)))
    value_raw = normal_values(splits[2], (TOKENS, D), 1.0, 6.0, ((0, 8), (1, 4)))
    featurizer = normal_values(splits[3], (3, TAPS, D), TAPS ** -0.5, 2.0, ((2, 4),), jnp.float32)
    filter_taps = draw_filter_taps(jax.random.fold_in(splits[6], 71), 0)
    cotangent = normal_values(splits[5], (TOKENS, D), 1.0, 6.0, ((0, 8), (1, 4)))
    return {"query_raw": query_raw, "key_raw": key_raw, "value_raw": value_raw, "featurizer": featurizer, "filter_taps": filter_taps, "cotangent": cotangent}


def featurize(raw, weight):
    signal = raw.astype(jnp.float32)
    padded = jnp.pad(signal, ((TAPS - 1, 0), (0, 0)))
    total = jnp.zeros_like(signal)
    for lag_index in range(TAPS):
        start = TAPS - 1 - lag_index
        total = total + weight[lag_index][None, :] * padded[start:start + TOKENS]
    return total


def unfeaturize(grad, weight):
    padded = jnp.pad(grad, ((0, TAPS - 1), (0, 0)))
    total = jnp.zeros_like(grad)
    for lag_index in range(TAPS):
        total = total + weight[lag_index][None, :] * padded[lag_index:lag_index + TOKENS]
    return total


def weight_terms(grad, raw):
    padded = jnp.pad(raw.astype(jnp.float32), ((TAPS - 1, 0), (0, 0)))
    terms = []
    for lag_index in range(TAPS):
        start = TAPS - 1 - lag_index
        terms.append(jnp.sum(grad * padded[start:start + TOKENS], axis=0))
    return jnp.stack(terms)


def reference(query_raw, key_raw, value_raw, featurizer, filter_taps, cotangent):
    feat_query = featurize(query_raw, featurizer[0])
    feat_key = featurize(key_raw, featurizer[1])
    feat_value = featurize(value_raw, featurizer[2])
    mixer = (feat_key * feat_value).astype(jnp.bfloat16)
    upstream = cotangent.astype(jnp.float32)
    gate = (upstream * feat_query).astype(jnp.bfloat16)
    block_width = math.gcd(D, 256)
    full_len = 2 * TOKENS

    def to_blocks(array):
        return array.astype(jnp.float32).T.reshape(D // block_width, block_width, TOKENS)

    def from_blocks(array):
        return array.reshape(D, TOKENS).T

    def per_block(items):
        mix_block, taps_block, gate_block = items
        mix_spec = jnp.fft.rfft(mix_block, n=full_len, axis=-1)
        taps_spec = jnp.fft.rfft(taps_block, n=full_len, axis=-1)
        gate_spec = jnp.fft.rfft(gate_block, n=full_len, axis=-1)
        conv_block = jnp.fft.irfft(taps_spec * mix_spec, n=full_len, axis=-1)[:, :TOKENS]
        mix_grad_block = jnp.fft.irfft(jnp.conj(taps_spec) * gate_spec, n=full_len, axis=-1)[:, :TOKENS]
        taps_grad_block = jnp.fft.irfft(jnp.conj(mix_spec) * gate_spec, n=full_len, axis=-1)[:, :TOKENS]
        return conv_block, mix_grad_block, taps_grad_block

    conv, mixer_grad, taps_grad = lax.map(per_block, (to_blocks(mixer), to_blocks(filter_taps), to_blocks(gate)))
    scale = TOKENS ** -0.5
    conv = from_blocks(conv).astype(jnp.bfloat16)
    mixer_grad = from_blocks(mixer_grad).astype(jnp.bfloat16)
    filter_grad = from_blocks(taps_grad).astype(jnp.float32) * scale
    conv_float = conv.astype(jnp.float32)
    mixed = (feat_query * conv_float).astype(jnp.bfloat16)
    mix_grad_float = mixer_grad.astype(jnp.float32)
    query_feat_grad = upstream * conv_float
    key_feat_grad = mix_grad_float * feat_value
    value_feat_grad = mix_grad_float * feat_key
    query_grad = unfeaturize(query_feat_grad, featurizer[0]).astype(jnp.bfloat16)
    key_grad = unfeaturize(key_feat_grad, featurizer[1]).astype(jnp.bfloat16)
    value_grad = unfeaturize(value_feat_grad, featurizer[2]).astype(jnp.bfloat16)
    featurizer_grad = jnp.stack([
        weight_terms(query_feat_grad, query_raw),
        weight_terms(key_feat_grad, key_raw),
        weight_terms(value_feat_grad, value_raw),
    ]) * scale
    return mixed, query_grad, key_grad, value_grad, filter_grad, featurizer_grad
```

```python
import functools
import math

import jax
import jax.numpy as jnp
import numpy as np
from jax import lax
from jax.experimental import pallas as pl
from jax.experimental.pallas import tpu as pltpu
from jax.sharding import PartitionSpec as P

TAPS = 7


exact_mode = lax.Precision.HIGHEST


def passed_along(value, axis, steps):
    count = lax.axis_size(axis)
    initial, last = (max(0, -steps), min(count, count - steps))
    return lax.ppermute(value, axis, [(source, source + steps) for source in range(initial, last)])


def spectrum_tables(half_rows, tile_width):
    full_rows = 2 * half_rows
    length_full = full_rows * tile_width
    row_index = jnp.arange(full_rows, dtype=jnp.int32)
    col_index = jnp.arange(tile_width, dtype=jnp.int32)
    outer_angle = (
        2.0
        * math.pi
        / full_rows
        * (row_index[:, None] * row_index[None, :] % full_rows).astype(jnp.float32)
    )
    twist_angle = (
        2.0
        * math.pi
        / length_full
        * (row_index[:, None] * col_index[None, :] % length_full).astype(jnp.float32)
    )
    inner_angle = (
        2.0
        * math.pi
        / tile_width
        * (col_index[:, None] * col_index[None, :] % tile_width).astype(jnp.float32)
    )
    return (
        jnp.cos(outer_angle),
        -jnp.sin(outer_angle),
        jnp.cos(twist_angle),
        -jnp.sin(twist_angle),
        jnp.cos(inner_angle),
        -jnp.sin(inner_angle),
    )


def right_product(left, table):
    return jnp.einsum("ckm,mj->ckj", left, table, precision=exact_mode)


def to_spectrum(signal, tables):
    outer_re, outer_im, twist_re, twist_im, inner_re, inner_im = tables
    half_rows = outer_re.shape[0] // 2
    tile_width = inner_re.shape[0]
    blocks = signal.reshape(signal.shape[0], half_rows, tile_width)
    section_re = jnp.einsum("kn,cnm->ckm", outer_re[:, :half_rows], blocks, precision=exact_mode)
    section_im = jnp.einsum("kn,cnm->ckm", outer_im[:, :half_rows], blocks, precision=exact_mode)
    turned_re = section_re * twist_re - section_im * twist_im
    turned_im = section_re * twist_im + section_im * twist_re
    spec_re = right_product(turned_re, inner_re) - right_product(turned_im, inner_im)
    spec_im = right_product(turned_re, inner_im) + right_product(turned_im, inner_re)
    return (spec_re, spec_im)


def from_spectrum(spectrum, tables):
    outer_re, outer_im, twist_re, twist_im, inner_re, inner_im = tables
    half_rows = outer_re.shape[0] // 2
    tile_width = inner_re.shape[0]
    spec_re, spec_im = spectrum
    back_re = right_product(spec_re, inner_re) + right_product(spec_im, inner_im)
    back_im = right_product(spec_im, inner_re) - right_product(spec_re, inner_im)
    untwist_re = back_re * twist_re + back_im * twist_im
    untwist_im = back_im * twist_re - back_re * twist_im
    signal = jnp.einsum("nk,ckm->cnm", outer_re[:half_rows], untwist_re, precision=exact_mode)
    signal = signal + jnp.einsum(
        "nk,ckm->cnm", outer_im[:half_rows], untwist_im, precision=exact_mode
    )
    return signal.reshape(signal.shape[0], half_rows * tile_width) / (2.0 * half_rows * tile_width)


def times_spectrum(first, second):
    return (
        first[0] * second[0] - first[1] * second[1],
        first[0] * second[1] + first[1] * second[0],
    )


def conj_times(first, second):
    return (
        first[0] * second[0] + first[1] * second[1],
        first[0] * second[1] - first[1] * second[0],
    )


def featurize(padded, weight, tok_rows):
    total = jnp.zeros((tok_rows, padded.shape[1]), jnp.float32)
    for lag_index in range(TAPS):
        start = TAPS - 1 - lag_index
        total = total + weight[lag_index][None, :] * padded[start : start + tok_rows]
    return total


def unfeaturize(extended, weight, tok_rows):
    total = jnp.zeros((tok_rows, extended.shape[1]), jnp.float32)
    for lag_index in range(TAPS):
        total = total + weight[lag_index][None, :] * extended[lag_index : lag_index + tok_rows]
    return total


def weight_terms(grad, padded, tok_rows):
    terms = []
    for lag_index in range(TAPS):
        start = TAPS - 1 - lag_index
        terms.append(jnp.sum(grad * padded[start : start + tok_rows], axis=0))
    return jnp.stack(terms)


def on_device_large(query_raw, key_raw, value_raw, featurizer, filter_taps, cotangent):
    tok_rows = query_raw.shape[0]
    lag_rows = TAPS - 1
    cut_start = tok_rows - lag_rows
    seq_count = lax.axis_size("seq")
    ch_count = lax.axis_size("ch")
    rim_query, rim_key, rim_value = passed_along(
        (query_raw[cut_start:], key_raw[cut_start:], value_raw[cut_start:]), "seq", 1
    )
    padded_query = jnp.concatenate([rim_query, query_raw], axis=0).astype(jnp.float32)
    padded_key = jnp.concatenate([rim_key, key_raw], axis=0).astype(jnp.float32)
    padded_value = jnp.concatenate([rim_value, value_raw], axis=0).astype(jnp.float32)
    feat_query = featurize(padded_query, featurizer[0], tok_rows)
    feat_key = featurize(padded_key, featurizer[1], tok_rows)
    feat_value = featurize(padded_value, featurizer[2], tok_rows)
    mixer = (feat_key * feat_value).astype(jnp.bfloat16)
    mix_cols = lax.all_to_all(mixer.T, "seq", split_axis=0, concat_axis=1, tiled=True)
    chan_total, row_part = (filter_taps.shape[1], filter_taps.shape[0])
    block_width = chan_total // (seq_count * ch_count)
    ordered = filter_taps.T.reshape(ch_count, seq_count, block_width, row_part)
    ordered = jnp.transpose(ordered, (1, 0, 2, 3)).reshape(chan_total, row_part)
    taps_cols = lax.all_to_all(ordered, ("seq", "ch"), split_axis=0, concat_axis=1, tiled=True)
    length_full = mix_cols.shape[1]
    tables = spectrum_tables(length_full // 128, 128)
    mix_spec = to_spectrum(mix_cols.astype(jnp.float32), tables)
    taps_spec = to_spectrum(taps_cols.astype(jnp.float32), tables)
    conv_cols = from_spectrum(times_spectrum(taps_spec, mix_spec), tables).astype(jnp.bfloat16)
    conv_rows = lax.all_to_all(conv_cols, "seq", split_axis=1, concat_axis=0, tiled=True).T
    conv_float = conv_rows.astype(jnp.float32)
    mixed = (feat_query * conv_float).astype(jnp.bfloat16)
    upstream = cotangent.astype(jnp.float32)
    gate = (upstream * feat_query).astype(jnp.bfloat16)
    gate_cols = lax.all_to_all(gate.T, "seq", split_axis=0, concat_axis=1, tiled=True)
    gate_spec = to_spectrum(gate_cols.astype(jnp.float32), tables)
    scale = length_full ** (-0.5)
    mix_grad_cols = from_spectrum(conj_times(taps_spec, gate_spec), tables).astype(jnp.bfloat16)
    taps_grad_cols = from_spectrum(conj_times(mix_spec, gate_spec), tables) * scale
    mix_back = lax.all_to_all(mix_grad_cols, "seq", split_axis=1, concat_axis=0, tiled=True)
    mix_grad_float = mix_back.T.astype(jnp.float32)
    joint_back = lax.all_to_all(
        taps_grad_cols, ("seq", "ch"), split_axis=1, concat_axis=0, tiled=True
    )
    block_width = joint_back.shape[0] // (seq_count * ch_count)
    row_part = joint_back.shape[1]
    unordered = joint_back.reshape(seq_count, ch_count, block_width, row_part)
    unordered = jnp.transpose(unordered, (1, 0, 2, 3)).reshape(joint_back.shape[0], row_part)
    filter_grad = unordered.T
    query_feat_grad = upstream * conv_float
    key_feat_grad = mix_grad_float * feat_value
    value_feat_grad = mix_grad_float * feat_key
    next_query, next_key, next_value = passed_along(
        (query_feat_grad[:lag_rows], key_feat_grad[:lag_rows], value_feat_grad[:lag_rows]),
        "seq",
        -1,
    )
    query_grad = unfeaturize(
        jnp.concatenate([query_feat_grad, next_query], axis=0), featurizer[0], tok_rows
    )
    key_grad = unfeaturize(
        jnp.concatenate([key_feat_grad, next_key], axis=0), featurizer[1], tok_rows
    )
    value_grad = unfeaturize(
        jnp.concatenate([value_feat_grad, next_value], axis=0), featurizer[2], tok_rows
    )
    partial_terms = jnp.stack(
        [
            weight_terms(query_feat_grad, padded_query, tok_rows),
            weight_terms(key_feat_grad, padded_key, tok_rows),
            weight_terms(value_feat_grad, padded_value, tok_rows),
        ]
    )
    featurizer_grad = lax.psum(partial_terms, "seq") * scale
    return (
        mixed,
        query_grad.astype(jnp.bfloat16),
        key_grad.astype(jnp.bfloat16),
        value_grad.astype(jnp.bfloat16),
        filter_grad,
        featurizer_grad,
    )


LANES = 128
HALO = 16
STEP = 32
MESH = pl.DeviceIdType.MESH


def angle_tables(length):
    full = 2 * length
    col = np.arange(length)
    coarse = np.arange(length // STEP + 1) * STEP
    coarse = 2.0 * np.pi / full * ((coarse[:, None] * col[None, :LANES]) % full)
    fine = 2.0 * np.pi / full * ((np.arange(STEP)[:, None] * col[None, :]) % full)
    return [
        np.asarray(part, np.float32)
        for part in (np.cos(coarse), np.sin(coarse), np.cos(fine), np.sin(fine))
    ]


def split_parts(value):
    high = value.astype(jnp.bfloat16)
    return high, (value - high.astype(jnp.float32)).astype(jnp.bfloat16)


def matmul(left, right):
    return jnp.dot(left, right, preferred_element_type=jnp.float32)


def swapped(value):
    return pltpu.roll(value, LANES // 2, axis=1)


def low_lanes(rows):
    return lax.broadcasted_iota(jnp.int32, (rows, LANES), 1) < LANES // 2


def operator_kernel(
    dims,
    q_ref, k_ref, v_ref, w_ref, taps_ref, cot_ref, ac_ref, as_ref, bc_ref, bs_ref,
    mixed_ref, qg_ref, kg_ref, vg_ref, fgrad_ref, wgrad_ref,
    ext, feat, grads, tab, taps_rx, mg_tx, mg_rx, taps_in, hspec, spec, conv_tx, conv_rx,
    filt_tx, filt_rx, part_rx,
    halo_send, halo_recv, taps_send, taps_recv, mg_send, mg_recv,
    conv_send, conv_recv, filt_send, filt_recv, part_send, part_recv,
):
    seq_count, ch_count, tok, width = dims
    count = seq_count * ch_count
    length = seq_count * tok
    tiles = width // LANES
    rows_f = length // count
    half_f = rows_f // 2
    ext_rows = tok + HALO
    f32 = jnp.float32
    seq = lax.axis_index("seq")
    ch = lax.axis_index("ch")
    me = seq * ch_count + ch
    scale = length ** (-0.5)

    def place(flat):
        return lax.div(flat, ch_count), lax.rem(flat, ch_count)

    def peer(step):
        return lax.rem(me + step, count)

    def lane_ds(tile):
        return pl.ds(pl.multiple_of(tile * LANES, LANES), LANES)

    barrier = pltpu.get_barrier_semaphore()

    @pl.loop(1, count)
    def _(step):
        pl.semaphore_signal(barrier, inc=1, device_id=place(peer(step)), device_id_type=MESH)

    own = (q_ref, k_ref, v_ref, cot_ref)
    for i, ref in enumerate(own):
        ext[i, HALO : HALO + tok, :] = ref[...]

    @pl.when(seq == 0)
    def _():
        ext[:, 0:HALO, :] = jnp.zeros((4, HALO, width), jnp.bfloat16)

    @pl.when(seq == seq_count - 1)
    def _():
        ext[:, HALO + tok :, :] = jnp.zeros((4, HALO, width), jnp.bfloat16)

    def make_tables(first, last):
        @pl.loop(first, last)
        def _(a):
            rows = pl.ds(pl.multiple_of(a * STEP, STEP), STEP)
            ac = jnp.broadcast_to(ac_ref[pl.ds(a, 1), :], (STEP, LANES))
            an = jnp.broadcast_to(as_ref[pl.ds(a, 1), :], (STEP, LANES))
            for j in range(length // LANES):
                cols = slice(j * LANES, (j + 1) * LANES)
                bc, bs = bc_ref[:, cols], bs_ref[:, cols]
                tab[0, rows, cols], tab[1, rows, cols] = split_parts(ac * bc - an * bs)
                tab[2, rows, cols], tab[3, rows, cols] = split_parts(an * bc + ac * bs)

    blocks = length // STEP + 1
    early = blocks // 2
    make_tables(0, early)
    pl.semaphore_wait(barrier, count - 1)

    def halo_copy(src, dst, i, to):
        return pltpu.make_async_remote_copy(
            src_ref=src, dst_ref=dst, send_sem=halo_send.at[i], recv_sem=halo_recv.at[i],
            device_id=(to, ch), device_id_type=MESH,
        )

    def up_copy(i):
        return halo_copy(own[i].at[tok - HALO :], ext.at[i, 0:HALO], i, seq + 1)

    def down_copy(i):
        return halo_copy(own[i].at[0:HALO], ext.at[i, HALO + tok :], 3 + i, seq - 1)

    @pl.when(seq < seq_count - 1)
    def _():
        for i in range(3):
            up_copy(i).start()

    @pl.when(seq > 0)
    def _():
        for i in range(4):
            down_copy(i).start()

    def taps_copy(step):
        to_seq, to_ch = place(peer(step))
        return pltpu.make_async_remote_copy(
            src_ref=taps_ref.at[:, lane_ds(to_ch * tiles + lax.div(to_seq, 2))],
            dst_ref=taps_rx.at[me], send_sem=taps_send.at[step], recv_sem=taps_recv.at[step],
            device_id=(to_seq, to_ch), device_id_type=MESH,
        )

    @pl.loop(1, count)
    def _(step):
        taps_copy(step).start()

    taps_rx[me] = taps_ref[:, lane_ds(ch * tiles + lax.div(seq, 2))]

    @pl.when(seq > 0)
    def _():
        for i in range(3):
            up_copy(i).wait_recv()

    @pl.when(seq < seq_count - 1)
    def _():
        for i in range(4):
            down_copy(i).wait_recv()

    def mg_copy(to):
        return pltpu.make_async_remote_copy(
            src_ref=mg_tx.at[to], dst_ref=mg_rx.at[seq], send_sem=mg_send.at[to],
            recv_sem=mg_recv.at[seq], device_id=(to, ch), device_id_type=MESH,
        )

    low_tok = low_lanes(tok)

    @pl.loop(0, tiles)
    def _(turn):
        tile = lax.rem(turn + lax.div(seq, 2), tiles)
        cols = lane_ds(tile)
        parts = []
        for i in range(3):
            raw = ext[i, :, cols].astype(f32)
            total = jnp.zeros((ext_rows, LANES), f32)
            for lag in range(TAPS):
                total = total + w_ref[i, lag : lag + 1, cols] * raw[HALO - lag : HALO - lag + ext_rows]
            feat[i, :, cols] = total
            parts.append(total[:tok])
        mix = parts[1] * parts[2]
        gate = ext[3, HALO : HALO + tok, cols].astype(f32) * parts[0]
        even = jnp.where(low_tok, mix, swapped(gate)).astype(jnp.bfloat16)
        odd = jnp.where(low_tok, swapped(mix), gate).astype(jnp.bfloat16)
        for side, value in ((0, even), (1, odd)):
            to = 2 * tile + side
            mg_tx[to] = value

            @pl.when(to != seq)
            def _():
                mg_copy(to).start()

            @pl.when(to == seq)
            def _():
                mg_rx[to] = value

    make_tables(early, blocks)

    @pl.loop(1, count)
    def _(step):
        taps_copy(step).wait_recv()

    odd_side = lax.rem(seq, 2)
    taps_all = taps_rx[...].reshape(length, LANES).astype(f32)
    side_of = jnp.where(low_lanes(length), 0, 1)
    taps_in[...] = jnp.where(side_of == odd_side, taps_all, swapped(taps_all)).astype(jnp.bfloat16)

    chunk = min(2 * LANES, length)

    def row_chunk(i):
        return pl.ds(pl.multiple_of(i * chunk, chunk), chunk)

    @pl.loop(0, length // chunk)
    def _(i):
        rows = row_chunk(i)
        hspec[0, rows, :] = matmul(tab[0, rows, :], taps_in[...]) + matmul(tab[1, rows, :], taps_in[...])
        hspec[1, rows, :] = matmul(tab[2, rows, :], taps_in[...]) + matmul(tab[3, rows, :], taps_in[...])

    def from_peer(copy_of, total, mine):
        @pl.loop(0, total)
        def _(source):
            @pl.when(source != mine)
            def _():
                copy_of(source).wait_recv()

    def mg_arrival(source):
        return pltpu.make_async_remote_copy(
            src_ref=mg_tx.at[source], dst_ref=mg_rx.at[source], send_sem=mg_send.at[source],
            recv_sem=mg_recv.at[source], device_id=(source, ch), device_id_type=MESH,
        )

    from_peer(mg_arrival, seq_count, seq)

    signals = mg_rx.at[...]
    low_chunk = low_lanes(chunk)

    @pl.loop(0, length // chunk)
    def _(i):
        rows = row_chunk(i)
        both = signals[...].reshape(length, LANES)
        xr = matmul(tab[0, rows, :], both) + matmul(tab[1, rows, :], both)
        xs = matmul(tab[2, rows, :], both) + matmul(tab[3, rows, :], both)
        bins = lax.broadcasted_iota(jnp.int32, (chunk, LANES), 0) + i * chunk
        weight = jnp.where(bins == 0, 0.5 / length, 1.0 / length)
        hr = hspec[0, rows, :]
        hs = hspec[1, rows, :]
        wr, ws = xr * weight, xs * weight
        turned = jnp.where(low_chunk, -hs, hs)
        pr = hr * wr + turned * ws
        ps = hr * ws - turned * wr
        other_r, other_s = swapped(xr), swapped(xs)
        fr = wr * other_r + ws * other_s
        fs = wr * other_s - ws * other_r
        for j, value in ((0, pr), (2, ps)):
            spec[j, rows, 0:LANES], spec[j + 1, rows, 0:LANES] = split_parts(value)
        for j, value in ((0, fr), (2, fs)):
            spec[j, rows, LANES:], spec[j + 1, rows, LANES:] = split_parts(value)

    sign_full = 1.0 - 2.0 * lax.rem(lax.broadcasted_iota(jnp.int32, (length, LANES), 0), 2).astype(f32)
    last_x = jnp.sum(mg_rx[...].reshape(length, LANES).astype(f32) * sign_full, axis=0, keepdims=True)
    last_h = jnp.sum(taps_in[...].astype(f32) * sign_full, axis=0, keepdims=True)
    half_weight = 0.5 / length
    last_conv = last_x * last_h * half_weight
    last_filt = last_x * swapped(jnp.broadcast_to(last_x, (8, LANES)))[0:1] * half_weight

    def conv_copy(to):
        return pltpu.make_async_remote_copy(
            src_ref=conv_tx.at[to], dst_ref=conv_rx.at[seq], send_sem=conv_send.at[to],
            recv_sem=conv_recv.at[seq], device_id=(to, ch), device_id_type=MESH,
        )

    def filt_copy(to):
        return pltpu.make_async_remote_copy(
            src_ref=filt_tx.at[to], dst_ref=filt_rx.at[me], send_sem=filt_send.at[to],
            recv_sem=filt_recv.at[me], device_id=place(to), device_id_type=MESH,
        )

    low_half = low_lanes(half_f)
    sign_ext = sign_full[:ext_rows]

    @pl.loop(0, seq_count)
    def _(turn):
        to = lax.rem(seq + 1 + turn, seq_count)
        rows = pl.ds(pl.multiple_of(to * tok, tok), ext_rows)
        out = jnp.zeros((ext_rows, 2 * LANES), f32)
        for j in (0, 2):
            high = tab[j, rows, :]
            out = out + matmul(high, spec[j]) + matmul(high, spec[j + 1]) + matmul(tab[j + 1, rows, :], spec[j])
        conv_tx[to] = (out[:, :LANES] + sign_ext * last_conv).astype(jnp.bfloat16)
        filt = (out[:, LANES:] + sign_ext * last_filt) * scale

        @pl.when(to != seq)
        def _():
            conv_copy(to).start()

        @pl.when(to == seq)
        def _():
            conv_rx[to] = conv_tx[to]

        for c in range(ch_count):
            top = filt[c * rows_f : c * rows_f + half_f]
            bottom = filt[c * rows_f + half_f : (c + 1) * rows_f]
            flat = to * ch_count + c
            filt_tx[flat] = jnp.where(low_half, top, swapped(bottom)).astype(jnp.bfloat16)

            @pl.when(flat != me)
            def _():
                filt_copy(flat).start()

            @pl.when(flat == me)
            def _():
                filt_rx[flat] = filt_tx[flat]

    def conv_arrival(source):
        return pltpu.make_async_remote_copy(
            src_ref=conv_tx.at[source], dst_ref=conv_rx.at[source], send_sem=conv_send.at[source],
            recv_sem=conv_recv.at[source], device_id=(source, ch), device_id_type=MESH,
        )

    from_peer(conv_arrival, seq_count, seq)
    low_ext = low_lanes(ext_rows)
    row_ext = lax.broadcasted_iota(jnp.int32, (ext_rows, LANES), 0)
    keep = jnp.logical_or(row_ext < tok, seq < seq_count - 1)

    @pl.loop(0, tiles)
    def _(tile):
        cols = lane_ds(tile)
        first = jnp.where(keep, conv_rx[2 * tile].astype(f32), 0.0)
        second = jnp.where(keep, conv_rx[2 * tile + 1].astype(f32), 0.0)
        conv = jnp.where(low_ext, first, swapped(second))
        mix_grad = jnp.where(low_ext, swapped(first), second)
        mixed_ref[:, cols] = (feat[0, :tok, cols] * conv[:tok]).astype(jnp.bfloat16)
        terms = (
            ext[3, HALO:, cols].astype(f32) * conv,
            mix_grad * feat[2, :, cols],
            mix_grad * feat[1, :, cols],
        )
        for i in range(3):
            grads[i, :, cols] = terms[i]
            raw = ext[i, :, cols].astype(f32)
            sums = [
                jnp.sum(terms[i][:tok] * raw[HALO - lag : HALO - lag + tok], axis=0, keepdims=True)
                for lag in range(TAPS)
            ]
            sums.append(jnp.zeros((1, LANES), f32))
            part_rx[seq, 8 * i : 8 * i + 8, cols] = jnp.concatenate(sums, axis=0)

    def part_copy(step):
        to = lax.rem(seq + step, seq_count)
        return pltpu.make_async_remote_copy(
            src_ref=part_rx.at[seq], dst_ref=part_rx.at[seq], send_sem=part_send.at[to],
            recv_sem=part_recv.at[seq], device_id=(to, ch), device_id_type=MESH,
        )

    @pl.loop(1, seq_count)
    def _(step):
        part_copy(step).start()

    @pl.loop(0, tiles)
    def _(tile):
        cols = lane_ds(tile)
        for i, ref in enumerate((qg_ref, kg_ref, vg_ref)):
            term = grads[i, :, cols]
            total = jnp.zeros((tok, LANES), f32)
            for lag in range(TAPS):
                total = total + w_ref[i, lag : lag + 1, cols] * term[lag : lag + tok]
            ref[:, cols] = total.astype(jnp.bfloat16)

    def filt_arrival(source):
        return pltpu.make_async_remote_copy(
            src_ref=filt_tx.at[source], dst_ref=filt_rx.at[source], send_sem=filt_send.at[source],
            recv_sem=filt_recv.at[source], device_id=place(source), device_id_type=MESH,
        )

    from_peer(filt_arrival, count, me)

    @pl.loop(0, ch_count * tiles)
    def _(tile):
        cols = lane_ds(tile)
        pair = lax.rem(tile, tiles)
        owner = lax.div(tile, tiles)
        first = filt_rx[2 * pair * ch_count + owner].astype(f32)
        second = filt_rx[(2 * pair + 1) * ch_count + owner].astype(f32)
        fgrad_ref[0:half_f, cols] = jnp.where(low_half, first, swapped(second))
        fgrad_ref[half_f:rows_f, cols] = jnp.where(low_half, swapped(first), second)

    def part_arrival(source):
        return pltpu.make_async_remote_copy(
            src_ref=part_rx.at[seq], dst_ref=part_rx.at[source], send_sem=part_send.at[source],
            recv_sem=part_recv.at[source], device_id=(source, ch), device_id_type=MESH,
        )

    from_peer(part_arrival, seq_count, seq)
    whole = part_rx[0]
    for source in range(1, seq_count):
        whole = whole + part_rx[source]
    whole = whole * scale
    for i in range(3):
        wgrad_ref[i] = whole[8 * i : 8 * i + TAPS]

    @pl.when(seq < seq_count - 1)
    def _():
        for i in range(3):
            up_copy(i).wait_send()

    @pl.when(seq > 0)
    def _():
        for i in range(4):
            down_copy(i).wait_send()

    @pl.loop(1, count)
    def _(step):
        taps_copy(step).wait_send()
        filt_copy(peer(step)).wait_send()

    @pl.loop(1, seq_count)
    def _(step):
        to = lax.rem(seq + step, seq_count)
        mg_copy(to).wait_send()
        conv_copy(to).wait_send()
        part_copy(step).wait_send()


def on_device(dims, *args):
    seq_count, ch_count, tok, width = dims
    count = seq_count * ch_count
    length = seq_count * tok
    half_f = length // count // 2
    bf16, f32 = jnp.bfloat16, jnp.float32
    vmem = pl.BlockSpec(memory_space=pltpu.VMEM)
    ext_rows = tok + HALO
    dma = pltpu.SemaphoreType.DMA
    out = jax.ShapeDtypeStruct((tok, width), bf16)
    return pl.pallas_call(
        functools.partial(operator_kernel, dims),
        out_shape=(
            out, out, out, out,
            jax.ShapeDtypeStruct((length // count, width * ch_count), f32),
            jax.ShapeDtypeStruct((3, TAPS, width), f32),
        ),
        in_specs=[vmem] * 10,
        out_specs=(vmem,) * 6,
        scratch_shapes=[
            pltpu.VMEM((4, tok + 2 * HALO, width), bf16),
            pltpu.VMEM((3, ext_rows, width), f32),
            pltpu.VMEM((3, ext_rows, width), f32),
            pltpu.VMEM((4, length + STEP, length), bf16),
            pltpu.VMEM((count, 2 * half_f, LANES), bf16),
            pltpu.VMEM((seq_count, tok, LANES), bf16),
            pltpu.VMEM((seq_count, tok, LANES), bf16),
            pltpu.VMEM((length, LANES), bf16),
            pltpu.VMEM((2, length, LANES), f32),
            pltpu.VMEM((4, length, 2 * LANES), bf16),
            pltpu.VMEM((seq_count, ext_rows, LANES), bf16),
            pltpu.VMEM((seq_count, ext_rows, LANES), bf16),
            pltpu.VMEM((count, half_f, LANES), bf16),
            pltpu.VMEM((count, half_f, LANES), bf16),
            pltpu.VMEM((seq_count, 24, width), f32),
            dma((7,)), dma((7,)), dma((count,)), dma((count,)),
            dma((seq_count,)), dma((seq_count,)), dma((seq_count,)), dma((seq_count,)),
            dma((count,)), dma((count,)), dma((seq_count,)), dma((seq_count,)),
        ],
        compiler_params=pltpu.CompilerParams(collective_id=0, has_side_effects=True),
    )(*args, *angle_tables(length))


def block_function(mesh, query_raw, filter_taps):
    seq_count, ch_count = mesh.shape["seq"], mesh.shape["ch"]
    tok, width = query_raw.shape
    length = seq_count * tok
    rows_f = filter_taps.shape[0]
    fits = (
        2 * width == seq_count * LANES
        and seq_count % 2 == 0
        and tok % LANES == 0
        and length % (2 * LANES) == 0
        and length <= 2048
        and rows_f % 32 == 0
    )
    if fits:
        return functools.partial(on_device, (seq_count, ch_count, tok, width))
    return on_device_large


def solution(mesh):
    def body(*args):
        return block_function(mesh, args[0], args[4])(*args)

    return jax.shard_map(
        body,
        mesh=mesh,
        in_specs=(
            P("seq", "ch"),
            P("seq", "ch"),
            P("seq", "ch"),
            P(None, None, "ch"),
            P(("seq", "ch"), None),
            P("seq", "ch"),
        ),
        out_specs=(
            P("seq", "ch"),
            P("seq", "ch"),
            P("seq", "ch"),
            P("seq", "ch"),
            P(("seq", "ch"), None),
            P(None, None, "ch"),
        ),
        check_vma=False,
    )
```

```python
import functools
import math

import jax
import jax.numpy as jnp
import numpy as np
from jax import lax
from jax.experimental import pallas as pl
from jax.experimental.pallas import tpu as pltpu
from jax.sharding import PartitionSpec as P

TAPS = 7


exact_mode = lax.Precision.HIGHEST


def passed_along(value, axis, steps):
    count = lax.axis_size(axis)
    initial, last = (max(0, -steps), min(count, count - steps))
    return lax.ppermute(value, axis, [(source, source + steps) for source in range(initial, last)])


def spectrum_tables(half_rows, tile_width):
    full_rows = 2 * half_rows
    length_full = full_rows * tile_width
    row_index = jnp.arange(full_rows, dtype=jnp.int32)
    col_index = jnp.arange(tile_width, dtype=jnp.int32)
    outer_angle = (
        2.0
        * math.pi
        / full_rows
        * (row_index[:, None] * row_index[None, :] % full_rows).astype(jnp.float32)
    )
    twist_angle = (
        2.0
        * math.pi
        / length_full
        * (row_index[:, None] * col_index[None, :] % length_full).astype(jnp.float32)
    )
    inner_angle = (
        2.0
        * math.pi
        / tile_width
        * (col_index[:, None] * col_index[None, :] % tile_width).astype(jnp.float32)
    )
    return (
        jnp.cos(outer_angle),
        -jnp.sin(outer_angle),
        jnp.cos(twist_angle),
        -jnp.sin(twist_angle),
        jnp.cos(inner_angle),
        -jnp.sin(inner_angle),
    )


def right_product(left, table):
    return jnp.einsum("ckm,mj->ckj", left, table, precision=exact_mode)


def to_spectrum(signal, tables):
    outer_re, outer_im, twist_re, twist_im, inner_re, inner_im = tables
    half_rows = outer_re.shape[0] // 2
    tile_width = inner_re.shape[0]
    blocks = signal.reshape(signal.shape[0], half_rows, tile_width)
    section_re = jnp.einsum("kn,cnm->ckm", outer_re[:, :half_rows], blocks, precision=exact_mode)
    section_im = jnp.einsum("kn,cnm->ckm", outer_im[:, :half_rows], blocks, precision=exact_mode)
    turned_re = section_re * twist_re - section_im * twist_im
    turned_im = section_re * twist_im + section_im * twist_re
    spec_re = right_product(turned_re, inner_re) - right_product(turned_im, inner_im)
    spec_im = right_product(turned_re, inner_im) + right_product(turned_im, inner_re)
    return (spec_re, spec_im)


def from_spectrum(spectrum, tables):
    outer_re, outer_im, twist_re, twist_im, inner_re, inner_im = tables
    half_rows = outer_re.shape[0] // 2
    tile_width = inner_re.shape[0]
    spec_re, spec_im = spectrum
    back_re = right_product(spec_re, inner_re) + right_product(spec_im, inner_im)
    back_im = right_product(spec_im, inner_re) - right_product(spec_re, inner_im)
    untwist_re = back_re * twist_re + back_im * twist_im
    untwist_im = back_im * twist_re - back_re * twist_im
    signal = jnp.einsum("nk,ckm->cnm", outer_re[:half_rows], untwist_re, precision=exact_mode)
    signal = signal + jnp.einsum(
        "nk,ckm->cnm", outer_im[:half_rows], untwist_im, precision=exact_mode
    )
    return signal.reshape(signal.shape[0], half_rows * tile_width) / (2.0 * half_rows * tile_width)


def times_spectrum(first, second):
    return (
        first[0] * second[0] - first[1] * second[1],
        first[0] * second[1] + first[1] * second[0],
    )


def conj_times(first, second):
    return (
        first[0] * second[0] + first[1] * second[1],
        first[0] * second[1] - first[1] * second[0],
    )


def featurize(padded, weight, tok_rows):
    total = jnp.zeros((tok_rows, padded.shape[1]), jnp.float32)
    for lag_index in range(TAPS):
        start = TAPS - 1 - lag_index
        total = total + weight[lag_index][None, :] * padded[start : start + tok_rows]
    return total


def unfeaturize(extended, weight, tok_rows):
    total = jnp.zeros((tok_rows, extended.shape[1]), jnp.float32)
    for lag_index in range(TAPS):
        total = total + weight[lag_index][None, :] * extended[lag_index : lag_index + tok_rows]
    return total


def weight_terms(grad, padded, tok_rows):
    terms = []
    for lag_index in range(TAPS):
        start = TAPS - 1 - lag_index
        terms.append(jnp.sum(grad * padded[start : start + tok_rows], axis=0))
    return jnp.stack(terms)


def on_device_large(query_raw, key_raw, value_raw, featurizer, filter_taps, cotangent):
    tok_rows = query_raw.shape[0]
    lag_rows = TAPS - 1
    cut_start = tok_rows - lag_rows
    seq_count = lax.axis_size("seq")
    ch_count = lax.axis_size("ch")
    rim_query, rim_key, rim_value = passed_along(
        (query_raw[cut_start:], key_raw[cut_start:], value_raw[cut_start:]), "seq", 1
    )
    padded_query = jnp.concatenate([rim_query, query_raw], axis=0).astype(jnp.float32)
    padded_key = jnp.concatenate([rim_key, key_raw], axis=0).astype(jnp.float32)
    padded_value = jnp.concatenate([rim_value, value_raw], axis=0).astype(jnp.float32)
    feat_query = featurize(padded_query, featurizer[0], tok_rows)
    feat_key = featurize(padded_key, featurizer[1], tok_rows)
    feat_value = featurize(padded_value, featurizer[2], tok_rows)
    mixer = (feat_key * feat_value).astype(jnp.bfloat16)
    mix_cols = lax.all_to_all(mixer.T, "seq", split_axis=0, concat_axis=1, tiled=True)
    chan_total, row_part = (filter_taps.shape[1], filter_taps.shape[0])
    block_width = chan_total // (seq_count * ch_count)
    ordered = filter_taps.T.reshape(ch_count, seq_count, block_width, row_part)
    ordered = jnp.transpose(ordered, (1, 0, 2, 3)).reshape(chan_total, row_part)
    taps_cols = lax.all_to_all(ordered, ("seq", "ch"), split_axis=0, concat_axis=1, tiled=True)
    length_full = mix_cols.shape[1]
    tables = spectrum_tables(length_full // 128, 128)
    mix_spec = to_spectrum(mix_cols.astype(jnp.float32), tables)
    taps_spec = to_spectrum(taps_cols.astype(jnp.float32), tables)
    conv_cols = from_spectrum(times_spectrum(taps_spec, mix_spec), tables).astype(jnp.bfloat16)
    conv_rows = lax.all_to_all(conv_cols, "seq", split_axis=1, concat_axis=0, tiled=True).T
    conv_float = conv_rows.astype(jnp.float32)
    mixed = (feat_query * conv_float).astype(jnp.bfloat16)
    upstream = cotangent.astype(jnp.float32)
    gate = (upstream * feat_query).astype(jnp.bfloat16)
    gate_cols = lax.all_to_all(gate.T, "seq", split_axis=0, concat_axis=1, tiled=True)
    gate_spec = to_spectrum(gate_cols.astype(jnp.float32), tables)
    scale = length_full ** (-0.5)
    mix_grad_cols = from_spectrum(conj_times(taps_spec, gate_spec), tables).astype(jnp.bfloat16)
    taps_grad_cols = from_spectrum(conj_times(mix_spec, gate_spec), tables) * scale
    mix_back = lax.all_to_all(mix_grad_cols, "seq", split_axis=1, concat_axis=0, tiled=True)
    mix_grad_float = mix_back.T.astype(jnp.float32)
    joint_back = lax.all_to_all(
        taps_grad_cols, ("seq", "ch"), split_axis=1, concat_axis=0, tiled=True
    )
    block_width = joint_back.shape[0] // (seq_count * ch_count)
    row_part = joint_back.shape[1]
    unordered = joint_back.reshape(seq_count, ch_count, block_width, row_part)
    unordered = jnp.transpose(unordered, (1, 0, 2, 3)).reshape(joint_back.shape[0], row_part)
    filter_grad = unordered.T
    query_feat_grad = upstream * conv_float
    key_feat_grad = mix_grad_float * feat_value
    value_feat_grad = mix_grad_float * feat_key
    next_query, next_key, next_value = passed_along(
        (query_feat_grad[:lag_rows], key_feat_grad[:lag_rows], value_feat_grad[:lag_rows]),
        "seq",
        -1,
    )
    query_grad = unfeaturize(
        jnp.concatenate([query_feat_grad, next_query], axis=0), featurizer[0], tok_rows
    )
    key_grad = unfeaturize(
        jnp.concatenate([key_feat_grad, next_key], axis=0), featurizer[1], tok_rows
    )
    value_grad = unfeaturize(
        jnp.concatenate([value_feat_grad, next_value], axis=0), featurizer[2], tok_rows
    )
    partial_terms = jnp.stack(
        [
            weight_terms(query_feat_grad, padded_query, tok_rows),
            weight_terms(key_feat_grad, padded_key, tok_rows),
            weight_terms(value_feat_grad, padded_value, tok_rows),
        ]
    )
    featurizer_grad = lax.psum(partial_terms, "seq") * scale
    return (
        mixed,
        query_grad.astype(jnp.bfloat16),
        key_grad.astype(jnp.bfloat16),
        value_grad.astype(jnp.bfloat16),
        filter_grad,
        featurizer_grad,
    )


LANES = 128
HALO = 16
STEP = 32
SPLIT = (TAPS + 1) // 2
PART_ROWS = 16
MESH = pl.DeviceIdType.MESH


def angle_tables(length):
    full = 2 * length
    col = np.arange(length)
    coarse = np.arange(length // STEP + 1) * STEP
    coarse = 2.0 * np.pi / full * ((coarse[:, None] * col[None, :LANES]) % full)
    fine = 2.0 * np.pi / full * ((np.arange(STEP)[:, None] * col[None, :]) % full)
    return [
        np.asarray(part, np.float32)
        for part in (np.cos(coarse), np.sin(coarse), np.cos(fine), np.sin(fine))
    ]


def split_parts(value):
    high = value.astype(jnp.bfloat16)
    return high, (value - high.astype(jnp.float32)).astype(jnp.bfloat16)


def matmul(left, right):
    return jnp.dot(left, right, preferred_element_type=jnp.float32)


def swapped(value):
    return pltpu.roll(value, LANES // 2, axis=1)


def low_lanes(rows):
    return lax.broadcasted_iota(jnp.int32, (rows, LANES), 1) < LANES // 2


def operator_kernel(
    dims,
    q_ref, k_ref, v_ref, w_ref, taps_ref, cot_ref, ac_ref, as_ref, bc_ref, bs_ref,
    mixed_ref, qg_ref, kg_ref, vg_ref, fgrad_ref, wgrad_ref,
    ext, feat, grads, tab, taps_tx, taps_rx, mg_tx, mg_rx, taps_in, hspec, spec, conv_tx, conv_rx,
    filt_tx, filt_rx, part_tx, part_rx, sums_rx,
    halo_send, halo_recv, taps_send, taps_recv, mg_send, mg_recv,
    conv_send, conv_recv, filt_send, filt_recv, part_send, part_recv, sum_send, sum_recv,
):
    seq_count, ch_count, tok, width = dims
    count = seq_count * ch_count
    length = seq_count * tok
    tiles = width // LANES
    rows_f = length // count
    half_f = rows_f // 2
    ext_rows = tok + HALO
    f32 = jnp.float32
    seq = lax.axis_index("seq")
    ch = lax.axis_index("ch")
    me = seq * ch_count + ch
    scale = length ** (-0.5)

    def place(flat):
        return lax.div(flat, ch_count), lax.rem(flat, ch_count)

    def peer(step):
        return lax.rem(me + step, count)

    def lane_ds(tile):
        return pl.ds(pl.multiple_of(tile * LANES, LANES), LANES)

    barrier = pltpu.get_barrier_semaphore()

    @pl.loop(1, count)
    def _(step):
        pl.semaphore_signal(barrier, inc=1, device_id=place(peer(step)), device_id_type=MESH)

    low_half = low_lanes(half_f)

    @pl.loop(0, ch_count * tiles)
    def _(tile):
        cols = lane_ds(tile)
        top = taps_ref[0:half_f, cols].astype(f32)
        bottom = taps_ref[half_f:rows_f, cols].astype(f32)
        even_flat = 2 * lax.rem(tile, tiles) * ch_count + lax.div(tile, tiles)
        taps_tx[even_flat] = jnp.where(low_half, top, swapped(bottom)).astype(jnp.bfloat16)
        taps_tx[even_flat + ch_count] = jnp.where(low_half, swapped(top), bottom).astype(jnp.bfloat16)

    own = (q_ref, k_ref, v_ref, cot_ref)
    for i, ref in enumerate(own):
        ext[i, HALO : HALO + tok, :] = ref[...]

    @pl.when(seq == 0)
    def _():
        ext[:, 0:HALO, :] = jnp.zeros((4, HALO, width), jnp.bfloat16)

    @pl.when(seq == seq_count - 1)
    def _():
        ext[:, HALO + tok :, :] = jnp.zeros((4, HALO, width), jnp.bfloat16)

    def make_tables(first, last):
        @pl.loop(first, last)
        def _(a):
            rows = pl.ds(pl.multiple_of(a * STEP, STEP), STEP)
            ac = jnp.broadcast_to(ac_ref[pl.ds(a, 1), :], (STEP, LANES))
            an = jnp.broadcast_to(as_ref[pl.ds(a, 1), :], (STEP, LANES))
            for j in range(length // LANES):
                cols = slice(j * LANES, (j + 1) * LANES)
                bc, bs = bc_ref[:, cols], bs_ref[:, cols]
                tab[0, rows, cols], tab[1, rows, cols] = split_parts(ac * bc - an * bs)
                tab[2, rows, cols], tab[3, rows, cols] = split_parts(an * bc + ac * bs)

    blocks = length // STEP + 1
    early = blocks // 2
    make_tables(0, early)
    pl.semaphore_wait(barrier, count - 1)

    def halo_copy(src, dst, i, to):
        return pltpu.make_async_remote_copy(
            src_ref=src, dst_ref=dst, send_sem=halo_send.at[i], recv_sem=halo_recv.at[i],
            device_id=(to, ch), device_id_type=MESH,
        )

    def up_copy(i):
        return halo_copy(own[i].at[tok - HALO :], ext.at[i, 0:HALO], i, seq + 1)

    def down_copy(i):
        return halo_copy(own[i].at[0:HALO], ext.at[i, HALO + tok :], 3 + i, seq - 1)

    @pl.when(seq < seq_count - 1)
    def _():
        for i in range(3):
            up_copy(i).start()

    @pl.when(seq > 0)
    def _():
        for i in range(4):
            down_copy(i).start()

    def taps_copy(step):
        to_seq, to_ch = place(peer(step))
        return pltpu.make_async_remote_copy(
            src_ref=taps_tx.at[peer(step)],
            dst_ref=taps_rx.at[me], send_sem=taps_send.at[step], recv_sem=taps_recv.at[step],
            device_id=(to_seq, to_ch), device_id_type=MESH,
        )

    @pl.loop(1, count)
    def _(step):
        taps_copy(step).start()

    taps_rx[me] = taps_tx[me]

    @pl.when(seq > 0)
    def _():
        for i in range(3):
            up_copy(i).wait_recv()

    @pl.when(seq < seq_count - 1)
    def _():
        for i in range(4):
            down_copy(i).wait_recv()

    def mg_copy(to):
        return pltpu.make_async_remote_copy(
            src_ref=mg_tx.at[to], dst_ref=mg_rx.at[seq], send_sem=mg_send.at[to],
            recv_sem=mg_recv.at[seq], device_id=(to, ch), device_id_type=MESH,
        )

    low_tok = low_lanes(tok)

    @pl.loop(0, tiles)
    def _(turn):
        tile = lax.rem(turn + lax.div(seq, 2), tiles)
        cols = lane_ds(tile)
        parts = []
        for i in range(3):
            raw = ext[i, :, cols].astype(f32)
            total = jnp.zeros((ext_rows, LANES), f32)
            for lag in range(TAPS):
                total = total + w_ref[i, lag : lag + 1, cols] * raw[HALO - lag : HALO - lag + ext_rows]
            feat[i, :, cols] = total
            parts.append(total[:tok])
        mix = parts[1] * parts[2]
        gate = ext[3, HALO : HALO + tok, cols].astype(f32) * parts[0]
        even = jnp.where(low_tok, mix, swapped(gate)).astype(jnp.bfloat16)
        odd = jnp.where(low_tok, swapped(mix), gate).astype(jnp.bfloat16)
        for side, value in ((0, even), (1, odd)):
            to = 2 * tile + side
            mg_tx[to] = value

            @pl.when(to != seq)
            def _():
                mg_copy(to).start()

            @pl.when(to == seq)
            def _():
                mg_rx[to] = value

    make_tables(early, blocks)

    @pl.loop(1, count)
    def _(step):
        taps_copy(step).wait_recv()

    low_count = low_lanes(count * half_f)
    taps_all = taps_rx[...].reshape(count * half_f, LANES).astype(f32)
    taps_turned = swapped(taps_all)
    for side, pair in enumerate(((taps_all, taps_turned), (taps_turned, taps_all))):
        value = jnp.where(low_count, *pair).astype(jnp.bfloat16)
        taps_in[:, side * half_f : (side + 1) * half_f, :] = value.reshape(count, half_f, LANES)

    chunk = min(2 * LANES, length)

    def row_chunk(i):
        return pl.ds(pl.multiple_of(i * chunk, chunk), chunk)

    @pl.loop(0, length // chunk)
    def _(i):
        rows = row_chunk(i)
        hspec[0, rows, :] = matmul(tab[0, rows, :], taps_in[...].reshape(length, LANES)) + matmul(tab[1, rows, :], taps_in[...].reshape(length, LANES))
        hspec[1, rows, :] = matmul(tab[2, rows, :], taps_in[...].reshape(length, LANES)) + matmul(tab[3, rows, :], taps_in[...].reshape(length, LANES))

    def from_peer(copy_of, total, mine):
        @pl.loop(0, total)
        def _(source):
            @pl.when(source != mine)
            def _():
                copy_of(source).wait_recv()

    def mg_arrival(source):
        return pltpu.make_async_remote_copy(
            src_ref=mg_tx.at[source], dst_ref=mg_rx.at[source], send_sem=mg_send.at[source],
            recv_sem=mg_recv.at[source], device_id=(source, ch), device_id_type=MESH,
        )

    from_peer(mg_arrival, seq_count, seq)

    signals = mg_rx.at[...]
    low_chunk = low_lanes(chunk)

    @pl.loop(0, length // chunk)
    def _(i):
        rows = row_chunk(i)
        both = signals[...].reshape(length, LANES)
        xr = matmul(tab[0, rows, :], both) + matmul(tab[1, rows, :], both)
        xs = matmul(tab[2, rows, :], both) + matmul(tab[3, rows, :], both)
        bins = lax.broadcasted_iota(jnp.int32, (chunk, LANES), 0) + i * chunk
        weight = jnp.where(bins == 0, 0.5 / length, 1.0 / length)
        hr = hspec[0, rows, :]
        hs = hspec[1, rows, :]
        wr, ws = xr * weight, xs * weight
        turned = jnp.where(low_chunk, -hs, hs)
        pr = hr * wr + turned * ws
        ps = hr * ws - turned * wr
        other_r, other_s = swapped(xr), swapped(xs)
        fr = wr * other_r + ws * other_s
        fs = wr * other_s - ws * other_r
        for j, value in ((0, pr), (2, ps)):
            spec[j, rows, 0:LANES], spec[j + 1, rows, 0:LANES] = split_parts(value)
        for j, value in ((0, fr), (2, fs)):
            spec[j, rows, LANES:], spec[j + 1, rows, LANES:] = split_parts(value)

    sign_full = 1.0 - 2.0 * lax.rem(lax.broadcasted_iota(jnp.int32, (length, LANES), 0), 2).astype(f32)
    last_x = jnp.sum(mg_rx[...].reshape(length, LANES).astype(f32) * sign_full, axis=0, keepdims=True)
    last_h = jnp.sum(taps_in[...].reshape(length, LANES).astype(f32) * sign_full, axis=0, keepdims=True)
    half_weight = 0.5 / length
    last_conv = last_x * last_h * half_weight
    last_filt = last_x * swapped(jnp.broadcast_to(last_x, (8, LANES)))[0:1] * half_weight

    def conv_copy(to):
        return pltpu.make_async_remote_copy(
            src_ref=conv_tx.at[to], dst_ref=conv_rx.at[seq], send_sem=conv_send.at[to],
            recv_sem=conv_recv.at[seq], device_id=(to, ch), device_id_type=MESH,
        )

    def filt_copy(to):
        return pltpu.make_async_remote_copy(
            src_ref=filt_tx.at[to], dst_ref=filt_rx.at[me], send_sem=filt_send.at[to],
            recv_sem=filt_recv.at[me], device_id=place(to), device_id_type=MESH,
        )

    sign_ext = sign_full[:ext_rows]

    @pl.loop(0, seq_count)
    def _(turn):
        to = lax.rem(seq + 1 + turn, seq_count)
        rows = pl.ds(pl.multiple_of(to * tok, tok), ext_rows)
        out = jnp.zeros((ext_rows, 2 * LANES), f32)
        for j in (0, 2):
            high = tab[j, rows, :]
            out = out + matmul(high, spec[j]) + matmul(high, spec[j + 1]) + matmul(tab[j + 1, rows, :], spec[j])
        conv_tx[to] = (out[:, :LANES] + sign_ext * last_conv).astype(jnp.bfloat16)
        filt = (out[:, LANES:] + sign_ext * last_filt) * scale

        @pl.when(to != seq)
        def _():
            conv_copy(to).start()

        @pl.when(to == seq)
        def _():
            conv_rx[to] = conv_tx[to]

        for c in range(ch_count):
            top = filt[c * rows_f : c * rows_f + half_f]
            bottom = filt[c * rows_f + half_f : (c + 1) * rows_f]
            flat = to * ch_count + c
            filt_tx[flat] = jnp.where(low_half, top, swapped(bottom)).astype(jnp.bfloat16)


    filt_rx[me] = filt_tx[me]

    @pl.loop(1, count)
    def _(step):
        filt_copy(peer(step)).start()

    def conv_arrival(source):
        return pltpu.make_async_remote_copy(
            src_ref=conv_tx.at[source], dst_ref=conv_rx.at[source], send_sem=conv_send.at[source],
            recv_sem=conv_recv.at[source], device_id=(source, ch), device_id_type=MESH,
        )

    from_peer(conv_arrival, seq_count, seq)
    low_ext = low_lanes(ext_rows)
    row_ext = lax.broadcasted_iota(jnp.int32, (ext_rows, LANES), 0)
    keep = jnp.logical_or(row_ext < tok, seq < seq_count - 1)

    def part_copy(to):
        return pltpu.make_async_remote_copy(
            src_ref=part_tx.at[to], dst_ref=part_rx.at[seq], send_sem=part_send.at[to],
            recv_sem=part_recv.at[seq], device_id=(to, ch), device_id_type=MESH,
        )

    @pl.loop(0, tiles)
    def _(tile):
        cols = lane_ds(tile)
        first = jnp.where(keep, conv_rx[2 * tile].astype(f32), 0.0)
        second = jnp.where(keep, conv_rx[2 * tile + 1].astype(f32), 0.0)
        conv = jnp.where(low_ext, first, swapped(second))
        mix_grad = jnp.where(low_ext, swapped(first), second)
        mixed_ref[:, cols] = (feat[0, :tok, cols] * conv[:tok]).astype(jnp.bfloat16)
        terms = (
            ext[3, HALO:, cols].astype(f32) * conv,
            mix_grad * feat[2, :, cols],
            mix_grad * feat[1, :, cols],
        )
        lags = []
        for i in range(3):
            grads[i, :, cols] = terms[i]
            raw = ext[i, :, cols].astype(f32)
            sums = [
                jnp.sum(terms[i][:tok] * raw[HALO - lag : HALO - lag + tok], axis=0, keepdims=True)
                for lag in range(TAPS)
            ]
            lags.append(sums)
        for side in range(2):
            picked = [row for sums in lags for row in sums[side * SPLIT : (side + 1) * SPLIT]]
            picked.append(jnp.zeros((PART_ROWS - len(picked), LANES), f32))
            to = 2 * tile + side
            part_tx[to] = jnp.concatenate(picked, axis=0)

            @pl.when(to != seq)
            def _():
                part_copy(to).start()

            @pl.when(to == seq)
            def _():
                part_rx[to] = part_tx[to]

    @pl.loop(0, tiles)
    def _(tile):
        cols = lane_ds(tile)
        for i, ref in enumerate((qg_ref, kg_ref, vg_ref)):
            term = grads[i, :, cols]
            total = jnp.zeros((tok, LANES), f32)
            for lag in range(TAPS):
                total = total + w_ref[i, lag : lag + 1, cols] * term[lag : lag + tok]
            ref[:, cols] = total.astype(jnp.bfloat16)

    def part_arrival(source):
        return pltpu.make_async_remote_copy(
            src_ref=part_tx.at[source], dst_ref=part_rx.at[source], send_sem=part_send.at[source],
            recv_sem=part_recv.at[source], device_id=(source, ch), device_id_type=MESH,
        )

    from_peer(part_arrival, seq_count, seq)
    own_sum = part_rx[0]
    for source in range(1, seq_count):
        own_sum = own_sum + part_rx[source]
    sums_rx[seq] = own_sum * scale

    def sum_copy(to):
        return pltpu.make_async_remote_copy(
            src_ref=sums_rx.at[seq], dst_ref=sums_rx.at[seq], send_sem=sum_send.at[to],
            recv_sem=sum_recv.at[seq], device_id=(to, ch), device_id_type=MESH,
        )

    @pl.loop(1, seq_count)
    def _(step):
        sum_copy(lax.rem(seq + step, seq_count)).start()

    def filt_arrival(source):
        return pltpu.make_async_remote_copy(
            src_ref=filt_tx.at[source], dst_ref=filt_rx.at[source], send_sem=filt_send.at[source],
            recv_sem=filt_recv.at[source], device_id=place(source), device_id_type=MESH,
        )

    from_peer(filt_arrival, count, me)

    @pl.loop(0, ch_count * tiles)
    def _(tile):
        cols = lane_ds(tile)
        pair = lax.rem(tile, tiles)
        owner = lax.div(tile, tiles)
        first = filt_rx[2 * pair * ch_count + owner].astype(f32)
        second = filt_rx[(2 * pair + 1) * ch_count + owner].astype(f32)
        fgrad_ref[0:half_f, cols] = jnp.where(low_half, first, swapped(second))
        fgrad_ref[half_f:rows_f, cols] = jnp.where(low_half, swapped(first), second)

    def sum_arrival(source):
        return pltpu.make_async_remote_copy(
            src_ref=sums_rx.at[seq], dst_ref=sums_rx.at[source], send_sem=sum_send.at[source],
            recv_sem=sum_recv.at[source], device_id=(source, ch), device_id_type=MESH,
        )

    from_peer(sum_arrival, seq_count, seq)
    for tile in range(tiles):
        cols = slice(tile * LANES, (tile + 1) * LANES)
        for side in range(2):
            rows = min(SPLIT, TAPS - side * SPLIT)
            for i in range(3):
                wgrad_ref[i, side * SPLIT : side * SPLIT + rows, cols] = sums_rx[
                    2 * tile + side, i * rows : (i + 1) * rows
                ]

    @pl.when(seq < seq_count - 1)
    def _():
        for i in range(3):
            up_copy(i).wait_send()

    @pl.when(seq > 0)
    def _():
        for i in range(4):
            down_copy(i).wait_send()

    @pl.loop(1, count)
    def _(step):
        taps_copy(step).wait_send()
        filt_copy(peer(step)).wait_send()

    @pl.loop(1, seq_count)
    def _(step):
        to = lax.rem(seq + step, seq_count)
        mg_copy(to).wait_send()
        conv_copy(to).wait_send()
        part_copy(to).wait_send()
        sum_copy(to).wait_send()


def write_out(*refs):
    half = len(refs) // 2
    for source, target in zip(refs[:half], refs[half:]):
        target[...] = source[...]


def on_device(dims, *args):
    seq_count, ch_count, tok, width = dims
    count = seq_count * ch_count
    length = seq_count * tok
    half_f = length // count // 2
    bf16, f32 = jnp.bfloat16, jnp.float32
    vmem = pl.BlockSpec(memory_space=pltpu.VMEM)
    ext_rows = tok + HALO
    dma = pltpu.SemaphoreType.DMA
    out = jax.ShapeDtypeStruct((tok, width), bf16)
    outs = (
        out, out, out, out,
        jax.ShapeDtypeStruct((length // count, width * ch_count), f32),
        jax.ShapeDtypeStruct((3, TAPS, width), f32),
    )
    results = pl.pallas_call(
        functools.partial(operator_kernel, dims),
        out_shape=outs,
        in_specs=[vmem] * 10,
        out_specs=(vmem,) * 6,
        scratch_shapes=[
            pltpu.VMEM((4, tok + 2 * HALO, width), bf16),
            pltpu.VMEM((3, ext_rows, width), f32),
            pltpu.VMEM((3, ext_rows, width), f32),
            pltpu.VMEM((4, length + STEP, length), bf16),
            pltpu.VMEM((count, half_f, LANES), bf16),
            pltpu.VMEM((count, half_f, LANES), bf16),
            pltpu.VMEM((seq_count, tok, LANES), bf16),
            pltpu.VMEM((seq_count, tok, LANES), bf16),
            pltpu.VMEM((count, 2 * half_f, LANES), bf16),
            pltpu.VMEM((2, length, LANES), f32),
            pltpu.VMEM((4, length, 2 * LANES), bf16),
            pltpu.VMEM((seq_count, ext_rows, LANES), bf16),
            pltpu.VMEM((seq_count, ext_rows, LANES), bf16),
            pltpu.VMEM((count, half_f, LANES), bf16),
            pltpu.VMEM((count, half_f, LANES), bf16),
            pltpu.VMEM((seq_count, PART_ROWS, LANES), f32),
            pltpu.VMEM((seq_count, PART_ROWS, LANES), f32),
            pltpu.VMEM((seq_count, PART_ROWS, LANES), f32),
            dma((7,)), dma((7,)), dma((count,)), dma((count,)),
            dma((seq_count,)), dma((seq_count,)), dma((seq_count,)), dma((seq_count,)),
            dma((count,)), dma((count,)), dma((seq_count,)), dma((seq_count,)),
            dma((seq_count,)), dma((seq_count,)),
        ],
        compiler_params=pltpu.CompilerParams(collective_id=0, has_side_effects=True),
    )(*args, *angle_tables(length))
    return pl.pallas_call(
        write_out, out_shape=outs, in_specs=[vmem] * 6, out_specs=(vmem,) * 6
    )(*results)


def block_function(mesh, query_raw, filter_taps):
    seq_count, ch_count = mesh.shape["seq"], mesh.shape["ch"]
    tok, width = query_raw.shape
    length = seq_count * tok
    rows_f = filter_taps.shape[0]
    fits = (
        2 * width == seq_count * LANES
        and seq_count % 2 == 0
        and tok % LANES == 0
        and length % (2 * LANES) == 0
        and length <= 2048
        and rows_f % 32 == 0
    )
    if fits:
        return functools.partial(on_device, (seq_count, ch_count, tok, width))
    return on_device_large


def solution(mesh):
    def body(*args):
        return block_function(mesh, args[0], args[4])(*args)

    return jax.shard_map(
        body,
        mesh=mesh,
        in_specs=(
            P("seq", "ch"),
            P("seq", "ch"),
            P("seq", "ch"),
            P(None, None, "ch"),
            P(("seq", "ch"), None),
            P("seq", "ch"),
        ),
        out_specs=(
            P("seq", "ch"),
            P("seq", "ch"),
            P("seq", "ch"),
            P("seq", "ch"),
            P(("seq", "ch"), None),
            P(None, None, "ch"),
        ),
        check_vma=False,
    )
```
